32 devices in a mesh: patch: 8 (over z, y), sample: 4 (over x, core).
Axes of the slice: x: 2, y: 2, z: 4, core: 2. Of those that a mesh axis runs over, the one named last changes fastest.
Arguments:
- features: bfloat16 [4, 4096, 512], P('sample', 'patch'), may hold values from -600 to 600
- cotangent: bfloat16 [4, 4096, 512], P('sample', 'patch'), may hold values from -6 to 6
- weight_qkv: bfloat16 [512, 1536], replicated, may hold values from -5 to 5
- weight_out: bfloat16 [512, 512], replicated, may hold values from -0.25 to 0.25
- key_tiles: int32 [32, 8], replicated, may hold values from 0 to 31, as said below
- tile_valid: int32 [32, 8], replicated, may hold values from 0 to 1, as said below
Outputs:
- grad_features: bfloat16 [4, 4096, 512], P('sample', 'patch')
- grad_qkv: float32 [512, 1536], replicated
- grad_out: float32 [512, 512], replicated
The draws below stay inside these ranges and needn't reach their ends.
Inputs may be any that keep to these rules, and one draw needn't show every extreme that they name: `key_tiles`: row g names 8 distinct tile ids. A tile's patch is its id // 4. The first id is g itself, the next 3 are other tiles of g's patch, and the last 4 lie one each in the patches at offsets -2 to 2 other than 0 around the cycle of patches, in rising order of offset. Over the rows of one patch exactly 2 distinct tiles of each such neighbouring patch are named. `tile_valid`: column 0 is always 1.
All inputs are finite; a program needn't handle non-finite values.
Results may differ from the reference program's by a relative error of at most 0.0088.
Values may be sent and summed in bfloat16 or wider, within the bound.
No kernel may reach another device: no remote copies, remote signals or barrier semaphores. Data moves between devices by JAX's collectives and lax.ppermute only.
A program may use at most 192 MiB of HBM per device.

```python
import jax
import jax.numpy as jnp
from jax import lax

D = 512
HEADS = 4
TILE = 128
TILE_DEV = 4
NB = 8
REACH = 2
CAP = 2
SAMPLES = 4
TILES = 32
NODES = 4096


def draw_features(key, part):
    base = jnp.clip(jax.random.normal(jax.random.fold_in(key, 1), (SAMPLES, NODES, D), jnp.float32), -5.0, 5.0)
    return base.astype(jnp.bfloat16)


def draw_weight_qkv(key, part):
    first = jnp.clip(jax.random.normal(jax.random.fold_in(key, 5), (D, 3 * D), jnp.float32), -5.0, 5.0)
    return (first * D ** (-0.5)).astype(jnp.bfloat16)


def draw_key_tiles(key, part):
    patches = TILES // TILE_DEV
    patch_of = jnp.arange(TILES, dtype=jnp.int32) // TILE_DEV
    local = jnp.arange(TILES, dtype=jnp.int32) % TILE_DEV
    own_keys = jax.random.split(jax.random.fold_in(key, 11), TILES)
    others = jax.vmap(lambda single: jax.random.permutation(single, TILE_DEV - 1))(own_keys)[:, :NB - 1 - 2 * REACH]
    neighbours = (local[:, None] + 1 + others.astype(jnp.int32)) % TILE_DEV + patch_of[:, None] * TILE_DEV
    columns = [(patch_of * TILE_DEV + local)[:, None], neighbours]
    chosen_keys = jax.random.split(jax.random.fold_in(key, 12), patches * 2 * REACH)
    chosen = jax.vmap(lambda single: jax.random.permutation(single, TILE_DEV)[:CAP])(chosen_keys)
    chosen = chosen.astype(jnp.int32).reshape(patches, 2 * REACH, CAP)
    picked = jax.random.randint(jax.random.fold_in(key, 13), (TILES, 2 * REACH), 0, CAP, jnp.int32)
    picked = jnp.where(local[:, None] < CAP, local[:, None], picked)
    offsets = [shift_by for shift_by in range(-REACH, REACH + 1) if shift_by != 0]
    for offset_index, shift_by in enumerate(offsets):
        target = (patch_of + shift_by) % patches
        entry = chosen[patch_of, offset_index, picked[:, offset_index]]
        columns.append((target * TILE_DEV + entry)[:, None])
    return jnp.concatenate(columns, 1).astype(jnp.int32)


def draw_tile_valid(key, part):
    levels = jax.random.randint(jax.random.fold_in(key, 21), (TILES, NB), 0, 4, jnp.int32)
    flags = (levels > 0).astype(jnp.int32)
    return flags.at[:, 0].set(1)


def block_levels(stream_key, dims, shards, least, largest):
    def one(position, shards_of):
        steps = jax.random.uniform(jax.random.fold_in(jax.random.fold_in(stream_key, 6), position), (shards_of,), jnp.float32, least / len(shards), largest / len(shards))
        return jnp.repeat(jnp.exp(steps), dims[position] // shards_of).reshape((-1,) + (1,) * (len(dims) - position - 1))

    level = one(*shards[0])
    for cut in shards[1:]:
        level = level * one(*cut)
    return level


def noise(rng, dims, spread, reach, cuts=(), kind=jnp.bfloat16):
    entries = jax.random.normal(rng, dims, jnp.float32) * spread
    if len(cuts) > 0:
        entries = block_levels(rng, dims, cuts, -0.22, 0.18) * entries
    return jnp.clip(entries, min=-reach, max=reach).astype(kind)


def setup_inputs(seed: int = 0) -> dict:
    keys = jax.random.split(jax.random.key(seed), 7)
    features = draw_features(jax.random.fold_in(keys[6], 71), 0)
    cotangent = noise(keys[1], (SAMPLES, NODES, D), 1.0, 6.0, ((0, 4), (1, 8)))
    weight_qkv = draw_weight_qkv(jax.random.fold_in(keys[6], 71), 0)
    weight_out = noise(keys[3], (D, D), D ** -0.5, 0.25)
    key_tiles = draw_key_tiles(jax.random.fold_in(keys[6], 71), 0)
    tile_valid = draw_tile_valid(jax.random.fold_in(keys[6], 71), 0)
    return dict(features=features, cotangent=cotangent, weight_qkv=weight_qkv, weight_out=weight_out, key_tiles=key_tiles, tile_valid=tile_valid)


epsilon = 1e-06

def tile_backward(query_tile, pair_tiles, live_flags, grad_tile):
    row_count = query_tile.shape[0]
    model_width = query_tile.shape[1]
    head_width = model_width // HEADS
    scaling = head_width ** (-0.5)
    key_heads = pair_tiles[:, :, :model_width].reshape(-1, HEADS, head_width).astype(jnp.float32)
    value_heads = pair_tiles[:, :, model_width:].reshape(-1, HEADS, head_width).astype(jnp.float32)
    query_heads = query_tile.reshape(row_count, HEADS, head_width).astype(jnp.float32)
    grad_heads = grad_tile.reshape(row_count, HEADS, head_width).astype(jnp.float32)
    scores = jnp.einsum('qhd,khd->hqk', query_heads, key_heads) * scaling
    live_mask = jnp.repeat(live_flags > 0, pair_tiles.shape[1])
    scores = jnp.where(live_mask[None, None, :], scores, -jnp.inf)
    highest = lax.optimization_barrier(jnp.max(scores, -1, keepdims=True))
    expanded = jnp.exp(scores - highest)
    attention = expanded / lax.optimization_barrier(jnp.sum(expanded, -1, keepdims=True))
    attention_low = lax.optimization_barrier(attention.astype(jnp.bfloat16)).astype(jnp.float32)
    attended = jnp.einsum('hqk,khd->qhd', attention_low, value_heads).astype(jnp.bfloat16).reshape(row_count, model_width)
    dprob = jnp.einsum('qhd,khd->hqk', grad_heads, value_heads)
    centre = lax.optimization_barrier(jnp.sum(attention * dprob, -1, keepdims=True))
    dscore = lax.optimization_barrier((attention * (dprob - centre) * scaling).astype(jnp.bfloat16)).astype(jnp.float32)
    dquery = jnp.einsum('hqk,khd->qhd', dscore, key_heads).reshape(row_count, model_width)
    dkey = jnp.einsum('hqk,qhd->khd', dscore, query_heads).reshape(pair_tiles.shape[0], pair_tiles.shape[1], model_width)
    dvalue = jnp.einsum('hqk,qhd->khd', attention_low, grad_heads).reshape(pair_tiles.shape[0], pair_tiles.shape[1], model_width)
    return (attended, dquery, jnp.concatenate([dkey, dvalue], -1))

def reference(features, cotangent, weight_qkv, weight_out, key_tiles, tile_valid):
    factor = float(SAMPLES * NODES) ** (-0.5)
    total_qkv = jnp.zeros((D, 3 * D), jnp.float32)
    total_out = jnp.zeros((D, D), jnp.float32)
    results = []
    for sample in range(SAMPLES):
        inputs = features[sample].astype(jnp.float32)
        inverse = lax.rsqrt(lax.optimization_barrier(jnp.mean(inputs * inputs, -1, keepdims=True)) + epsilon)
        normed = inputs * inverse
        normed_low = normed.astype(jnp.bfloat16)
        projected = jnp.dot(normed_low, weight_qkv, preferred_element_type=jnp.float32).astype(jnp.bfloat16)
        queries = projected[:, :D].reshape(TILES, TILE, D)
        pair_all = projected[:, D:].reshape(TILES, TILE, 2 * D)
        grad_rows = cotangent[sample]
        grad_attended = jnp.dot(grad_rows, weight_out.T, preferred_element_type=jnp.float32).astype(jnp.bfloat16)
        grad_tiles = grad_attended.reshape(TILES, TILE, D)

        def advance(running, pieces):
            query_tile, slot_ids, live_flags, grad_tile = pieces
            attended, dquery, dpairs = tile_backward(query_tile, pair_all[slot_ids], live_flags, grad_tile)
            return (running.at[slot_ids].add(dpairs), (attended, dquery))
        start_sums = jnp.zeros((TILES, TILE, 2 * D), jnp.float32)
        totals, (attended_all, dquery_all) = lax.scan(advance, start_sums, (queries, key_tiles, tile_valid, grad_tiles))
        attended_rows = attended_all.reshape(NODES, D)
        grad_projected = jnp.concatenate([dquery_all.reshape(NODES, D), totals.reshape(NODES, 2 * D)], 1).astype(jnp.bfloat16)
        grad_normed = jnp.dot(grad_projected, weight_qkv.T, preferred_element_type=jnp.float32)
        grad_inputs = grad_rows.astype(jnp.float32) + inverse * (grad_normed - normed * lax.optimization_barrier(jnp.mean(grad_normed * normed, -1, keepdims=True)))
        results.append(grad_inputs.astype(jnp.bfloat16))
        total_qkv = total_qkv + jnp.dot(normed_low.T, grad_projected, preferred_element_type=jnp.float32)
        total_out = total_out + jnp.dot(attended_rows.T, grad_rows, preferred_element_type=jnp.float32)
    return (jnp.stack(results, 0), total_qkv * factor, total_out * factor)
```

```python
from functools import partial

import jax
import jax.numpy as jnp
from jax import lax
from jax.experimental import pallas as pl
from jax.experimental.pallas import tpu as pltpu
from jax.sharding import PartitionSpec as P

HEADS = 4
TILE = 128
NB = 8
REACH = 2
CAP = 2
OFFSETS = [shift_by for shift_by in range(-REACH, REACH + 1) if shift_by != 0]
LOCAL = NB - len(OFFSETS)
SLOTS = CAP * len(OFFSETS)
MASKED = -1e30
AXES = ("patch", "sample")

epsilon = 1e-06

VMEM = pl.BlockSpec(memory_space=pltpu.VMEM)
SMEM = pl.BlockSpec(memory_space=pltpu.SMEM)


def nn(a, b):
    return jnp.dot(a, b, preferred_element_type=jnp.float32)


def nt(a, b):
    return lax.dot_general(a, b, (((1,), (1,)), ((), ())), preferred_element_type=jnp.float32)


def tn(a, b):
    return lax.dot_general(a, b, (((0,), (0,)), ((), ())), preferred_element_type=jnp.float32)


def normalise(rows):
    inputs = rows.astype(jnp.float32)
    inverse = lax.rsqrt(jnp.mean(inputs * inputs, -1, keepdims=True) + epsilon)
    return inputs * inverse, inverse


def named_pair(tiles_ref, first_row, column, count):
    named = [tiles_ref[first_row + row, column] for row in range(count)]
    low = high = named[0]
    for entry in named[1:]:
        low = jnp.minimum(low, entry)
        high = jnp.maximum(high, entry)
    return low, high


def sent_rows(tiles_ref, position, patches, column, shift_by, tile_count):
    target = lax.rem(position - shift_by + patches, patches)
    pair = named_pair(tiles_ref, target * tile_count, LOCAL + column, tile_count)
    return [pl.multiple_of((entry - position * tile_count) * TILE, TILE) for entry in pair]


def pack_kernel(patches, tiles_ref, place_ref, features_ref, *packed_refs):
    position = place_ref[0]
    tile_count = features_ref.shape[0] // TILE
    for column, shift_by in enumerate(OFFSETS):
        rows = sent_rows(tiles_ref, position, patches, column, shift_by, tile_count)
        for slot, first in enumerate(rows):
            packed_refs[column][slot] = features_ref[pl.ds(first, TILE), :]


def front_kernel(
    features_ref, cotangent_ref, weight_qkv_ref, weight_out_ref, normed_ref, projected_ref, grad_ref
):
    normed = normalise(features_ref[...])[0].astype(jnp.bfloat16)
    normed_ref[...] = normed
    projected_ref[...] = nn(normed, weight_qkv_ref[...]).astype(jnp.bfloat16)
    grad_ref[...] = nt(cotangent_ref[...], weight_out_ref[...]).astype(jnp.bfloat16)


def main_kernel(
    tiles_ref,
    valid_ref,
    place_ref,
    projected_ref,
    grad_ref,
    halo_a,
    halo_b,
    halo_c,
    halo_d,
    weight_ref,
    back_a,
    back_b,
    back_c,
    back_d,
    grad_own_ref,
    gp_own_ref,
    gp_halo_ref,
    normed_halo_ref,
    attended_ref,
    pair_s,
    prob_s,
    dscore_s,
    dkey_s,
    dvalue_s,
):
    halos = (halo_a, halo_b, halo_c, halo_d)
    backs = (back_a, back_b, back_c, back_d)
    position = place_ref[0]
    rows_local, width = grad_ref.shape
    tile_count = rows_local // TILE
    head_width = width // HEADS
    scaling = head_width ** (-0.5)
    first_row = position * tile_count
    for column, halo in enumerate(halos):
        for slot in range(CAP):
            normed = normalise(halo[slot])[0].astype(jnp.bfloat16)
            normed_halo_ref[pl.ds((column * CAP + slot) * TILE, TILE), :] = normed

    lane_tile = lax.broadcasted_iota(jnp.int32, (1, TILE), 1) * 0
    biases = []
    slots = []
    for tile in range(tile_count):
        row = first_row + tile
        pieces = []
        for other in range(tile_count):
            flag = jnp.int32(0)
            for column in range(LOCAL):
                flag = flag + jnp.where(
                    tiles_ref[row, column] == first_row + other, valid_ref[row, column], 0
                )
            pieces.append(jnp.where(lane_tile + flag > 0, 0.0, MASKED))
        places = []
        for column in range(len(OFFSETS)):
            high = named_pair(tiles_ref, first_row, LOCAL + column, tile_count)[1]
            place = jnp.where(tiles_ref[row, LOCAL + column] == high, 1, 0)
            places.append(column * CAP + place)
            flag = valid_ref[row, LOCAL + column]
            pieces.append(jnp.where(lane_tile + flag > 0, 0.0, MASKED))
        biases.append(jnp.concatenate(pieces, 1))
        slots.append(places)

    def one_head(head, carry):
        lanes = pl.ds(pl.multiple_of(head * head_width, head_width), head_width)
        key_lanes = pl.ds(pl.multiple_of(width + head * head_width, head_width), head_width)
        value_lanes = pl.ds(pl.multiple_of(2 * width + head * head_width, head_width), head_width)
        both = jnp.concatenate([weight_ref[:, key_lanes], weight_ref[:, value_lanes]], 1)
        pair_s[...] = nn(normed_halo_ref[...], both).astype(jnp.bfloat16)
        keys = projected_ref[:, key_lanes]
        values = projected_ref[:, value_lanes]
        queries_t = projected_ref[:, lanes].T
        grads_t = grad_ref[:, lanes].T
        dkey_s[...] = jnp.zeros_like(dkey_s)
        dvalue_s[...] = jnp.zeros_like(dvalue_s)
        for tile in range(tile_count):
            rows = pl.ds(tile * TILE, TILE)
            query = projected_ref[rows, lanes]
            grad = grad_ref[rows, lanes]
            starts = [pl.multiple_of(place * TILE, TILE) for place in slots[tile]]
            key_all = jnp.concatenate(
                [keys] + [pair_s[pl.ds(start, TILE), :head_width] for start in starts], 0
            )
            value_all = jnp.concatenate(
                [values] + [pair_s[pl.ds(start, TILE), head_width:] for start in starts], 0
            )
            scores = nt(query, key_all) * scaling + biases[tile]
            highest = jnp.max(scores, -1, keepdims=True)
            expanded = jnp.exp(scores - highest)
            attention = expanded * (1.0 / jnp.sum(expanded, -1, keepdims=True))
            low = attention.astype(jnp.bfloat16)
            attended_ref[rows, lanes] = nn(low, value_all).astype(jnp.bfloat16)
            dprob = nt(grad, value_all)
            centre = jnp.sum(attention * dprob, -1, keepdims=True)
            dscore = (attention * (dprob - centre)).astype(jnp.bfloat16)
            gp_own_ref[rows, lanes] = (nn(dscore, key_all) * scaling).astype(jnp.bfloat16)
            prob_s[rows, :] = low[:, :rows_local]
            dscore_s[rows, :] = dscore[:, :rows_local]
            dkey_t = nn(queries_t[:, tile * TILE : (tile + 1) * TILE], dscore[:, rows_local:])
            dvalue_t = nn(grads_t[:, tile * TILE : (tile + 1) * TILE], low[:, rows_local:])
            for column, place in enumerate(slots[tile]):
                part = slice(column * TILE, (column + 1) * TILE)
                dkey_s[place] += dkey_t[:, part]
                dvalue_s[place] += dvalue_t[:, part]
        dkey_own = nn(queries_t, dscore_s[...]) * scaling
        gp_own_ref[:, key_lanes] = dkey_own.T.astype(jnp.bfloat16)
        gp_own_ref[:, value_lanes] = nn(grads_t, prob_s[...]).T.astype(jnp.bfloat16)
        for place in range(SLOTS):
            rows = pl.ds(place * TILE, TILE)
            gp_halo_ref[rows, lanes] = (dkey_s[place] * scaling).T.astype(jnp.bfloat16)
            gp_halo_ref[rows, key_lanes] = dvalue_s[place].T.astype(jnp.bfloat16)
        return carry

    lax.fori_loop(0, HEADS, one_head, 0)
    for column, back in enumerate(backs):
        rows = pl.ds(column * CAP * TILE, CAP * TILE)
        part = nt(gp_halo_ref[rows, :], weight_ref[:, width:]).astype(jnp.bfloat16)
        back[...] = part.reshape(back.shape)
    grad_own_ref[...] = nt(gp_own_ref[...], weight_ref[...])


def weight_kernel(
    place_ref, normed_ref, normed_halo_ref, gp_own_ref, gp_halo_ref, attended_ref, cotangent_ref, out_ref
):
    width = normed_ref.shape[1]
    half = width // 2
    first = pl.multiple_of(place_ref[1] * half, half)
    lanes = pl.ds(first, half)
    normed = normed_ref[:, lanes]
    out_ref[:, :width] = tn(normed, gp_own_ref[:, :width]).astype(out_ref.dtype)
    pairs = tn(normed, gp_own_ref[:, width:]) + tn(normed_halo_ref[:, lanes], gp_halo_ref[...])
    out_ref[:, width : 3 * width] = pairs.astype(out_ref.dtype)
    out_ref[:, 3 * width :] = tn(attended_ref[:, lanes], cotangent_ref[...]).astype(out_ref.dtype)


def input_kernel(
    patches,
    tiles_ref,
    place_ref,
    features_ref,
    cotangent_ref,
    grad_own_ref,
    back_a,
    back_b,
    back_c,
    back_d,
    out_ref,
    total_s,
):
    position = place_ref[0]
    tile_count = features_ref.shape[0] // TILE
    total_s[...] = grad_own_ref[...]
    for column, (shift_by, back) in enumerate(zip(OFFSETS, (back_a, back_b, back_c, back_d))):
        rows = sent_rows(tiles_ref, position, patches, column, shift_by, tile_count)
        for slot, first in enumerate(rows):
            total_s[pl.ds(first, TILE), :] += back[slot].astype(jnp.float32)
    normed, inverse = normalise(features_ref[...])
    total = total_s[...]
    centred = total - normed * jnp.mean(total * normed, -1, keepdims=True)
    out_ref[...] = (cotangent_ref[...].astype(jnp.float32) + inverse * centred).astype(out_ref.dtype)


def from_behind(value, steps):
    count = lax.axis_size("patch")
    pairs = [(source, (source + steps) % count) for source in range(count)]
    return lax.ppermute(value, "patch", pairs)


def exchange(value, flip, count):
    return lax.ppermute(value, AXES, [(source, source ^ flip) for source in range(count)])


def flips_of(bits):
    return [
        sum(((step >> place) & 1) << bit for place, bit in enumerate(bits))
        for step in range(1 << len(bits))
    ]


def digit_of(index, bits):
    return sum(((index >> bit) & 1) << place for place, bit in enumerate(bits))


def reduce_phase(value, index, bits, count):
    flips = flips_of(bits)
    digit = digit_of(index, bits)
    pieces = value.reshape(len(flips), value.shape[0] // len(flips), value.shape[1])
    received = [
        exchange(lax.dynamic_index_in_dim(pieces, digit ^ step, 0, False), flips[step], count)
        for step in range(1, len(flips))
    ]
    total = lax.dynamic_index_in_dim(pieces, digit, 0, False).astype(jnp.float32)
    for piece in received:
        total = total + piece.astype(jnp.float32)
    return total


def gather_phase(value, index, bits, count):
    flips = flips_of(bits)
    digit = digit_of(index, bits)
    pieces = [value] + [exchange(value, flip, count) for flip in flips[1:]]
    stacked = jnp.zeros((len(flips),) + value.shape, value.dtype)
    for step, piece in enumerate(pieces):
        stacked = lax.dynamic_update_index_in_dim(stacked, piece, digit ^ step, 0)
    return stacked.reshape(len(flips) * value.shape[0], value.shape[1])


def on_device(features, cotangent, weight_qkv, weight_out, key_tiles, tile_valid):
    patches = lax.axis_size("patch")
    samples = lax.axis_size("sample")
    count = patches * samples
    position = lax.axis_index("patch").astype(jnp.int32)
    index = position * samples + lax.axis_index("sample").astype(jnp.int32)
    rows_local, width = features.shape[1:]
    rows = features[0]
    grad_rows = cotangent[0]
    low = jnp.bfloat16

    def shape(*dims, kind=low):
        return jax.ShapeDtypeStruct(dims, kind)

    params = pltpu.CompilerParams(vmem_limit_bytes=60 * 1024 * 1024)
    place = jnp.stack([position, index & 1])
    packed = pl.pallas_call(
        partial(pack_kernel, patches),
        out_shape=[shape(CAP, TILE, width)] * len(OFFSETS),
        in_specs=[SMEM, SMEM, VMEM],
        out_specs=[VMEM] * len(OFFSETS),
        name="pack",
    )(key_tiles, place, rows)
    halos = [from_behind(piece, -shift_by) for piece, shift_by in zip(packed, OFFSETS)]
    normed_low, projected, grad_attended = pl.pallas_call(
        front_kernel,
        out_shape=[shape(rows_local, width), shape(rows_local, 3 * width), shape(rows_local, width)],
        in_specs=[VMEM] * 4,
        out_specs=[VMEM] * 3,
        compiler_params=params,
        cost_estimate=pl.CostEstimate(
            flops=8 * rows_local * width * width, bytes_accessed=6 << 20, transcendentals=0
        ),
        name="front",
    )(rows, grad_rows, weight_qkv, weight_out)
    halo_rows = SLOTS * TILE
    head_width = width // HEADS
    outs = pl.pallas_call(
        main_kernel,
        out_shape=[shape(CAP, TILE, width)] * len(OFFSETS)
        + [
            shape(rows_local, width, kind=jnp.float32),
            shape(rows_local, 3 * width),
            shape(halo_rows, 2 * width),
            shape(halo_rows, width),
            shape(rows_local, width),
        ],
        in_specs=[SMEM] * 3 + [VMEM] * 7,
        out_specs=[VMEM] * (len(OFFSETS) + 5),
        scratch_shapes=[
            pltpu.VMEM((halo_rows, 2 * head_width), low),
            pltpu.VMEM((rows_local, rows_local), low),
            pltpu.VMEM((rows_local, rows_local), low),
            pltpu.VMEM((SLOTS, head_width, TILE), jnp.float32),
            pltpu.VMEM((SLOTS, head_width, TILE), jnp.float32),
        ],
        compiler_params=params,
        name="attend",
    )(key_tiles, tile_valid, place, projected, grad_attended, *halos, weight_qkv)
    backs, (grad_own, gp_own, gp_halo, normed_halo, attended) = outs[:4], outs[4:]
    returned = [from_behind(piece, shift_by) for piece, shift_by in zip(backs, OFFSETS)]

    def weights(side, kind):
        return pl.pallas_call(
            weight_kernel,
            out_shape=shape(width // 2, 4 * width, kind=kind),
            in_specs=[SMEM] + [VMEM] * 6,
            out_specs=VMEM,
            compiler_params=params,
            cost_estimate=pl.CostEstimate(
                flops=5 * rows_local * width * width, bytes_accessed=8 << 20, transcendentals=0
            ),
            name="weights",
        )(
            jnp.stack([position, side]),
            normed_low,
            normed_halo,
            gp_own,
            gp_halo,
            attended,
            grad_rows,
        )

    side = index & 1
    sent = weights(1 - side, low)
    arrived = exchange(sent, 1, count)
    kept = weights(side, jnp.float32)
    total = kept + arrived.astype(jnp.float32)
    bit_count = count.bit_length() - 1
    phases = [list(range(bit, min(bit + 2, bit_count))) for bit in range(1, bit_count, 2)]
    for bits in phases:
        total = reduce_phase(total.astype(low), index, bits, count)
    factor = float(count * rows_local) ** (-0.5)
    gathered = (total * factor).astype(low)
    for bits in phases[::-1] + [[0]]:
        gathered = gather_phase(gathered, index, bits, count)
    grad_qkv = gathered[:, : 3 * width].astype(jnp.float32)
    grad_out = gathered[:, 3 * width :].astype(jnp.float32)
    grad_features = pl.pallas_call(
        partial(input_kernel, patches),
        out_shape=shape(rows_local, width),
        in_specs=[SMEM, SMEM] + [VMEM] * 7,
        out_specs=VMEM,
        scratch_shapes=[pltpu.VMEM((rows_local, width), jnp.float32)],
        compiler_params=params,
        cost_estimate=pl.CostEstimate(
            flops=20 * rows_local * width, bytes_accessed=4 << 20, transcendentals=0
        ),
        name="inputs",
    )(key_tiles, place, rows, grad_rows, grad_own, *returned)
    return (grad_features[None], grad_qkv, grad_out)


def solution(mesh):
    placed = (P("sample", "patch", None), P("sample", "patch", None), P(), P(), P(), P())
    return jax.shard_map(
        on_device,
        mesh=mesh,
        in_specs=placed,
        out_specs=(P("sample", "patch", None), P(), P()),
        check_vma=False,
    )
```

```python
from functools import partial

import jax
import jax.numpy as jnp
from jax import lax
from jax.experimental import pallas as pl
from jax.experimental.pallas import tpu as pltpu
from jax.sharding import PartitionSpec as P


HEADS = 4
TILE = 128
NB = 8
REACH = 2
CAP = 2
OFFSETS = [shift_by for shift_by in range(-REACH, REACH + 1) if shift_by != 0]
LOCAL = NB - len(OFFSETS)
SLOTS = CAP * len(OFFSETS)
MASKED = -1e30
CHUNK = 16
AXES = ("patch", "sample")

epsilon = 1e-06

VMEM = pl.BlockSpec(memory_space=pltpu.VMEM)
SMEM = pl.BlockSpec(memory_space=pltpu.SMEM)
ANY = pl.BlockSpec(memory_space=pl.ANY)


def nn(a, b):
    return jnp.dot(a, b, preferred_element_type=jnp.float32)


def nt(a, b):
    return lax.dot_general(a, b, (((1,), (1,)), ((), ())), preferred_element_type=jnp.float32)


def normalise(rows):
    inputs = rows.astype(jnp.float32)
    inverse = lax.rsqrt(jnp.mean(inputs * inputs, -1, keepdims=True) + epsilon)
    return inputs * inverse, inverse


def named_pair(tiles_ref, first_row, column, count):
    named = [tiles_ref[first_row + row, column] for row in range(count)]
    low = high = named[0]
    for entry in named[1:]:
        low = jnp.minimum(low, entry)
        high = jnp.maximum(high, entry)
    return low, high


def sent_rows(tiles_ref, position, patches, column, shift_by, tile_count):
    target = lax.rem(position - shift_by + patches, patches)
    pair = named_pair(tiles_ref, target * tile_count, LOCAL + column, tile_count)
    return [pl.multiple_of((entry - position * tile_count) * TILE, TILE) for entry in pair]


def pack_kernel(patches, tiles_ref, place_ref, features_ref, *packed_refs):
    position = place_ref[0]
    tile_count = features_ref.shape[0] // TILE
    for column, shift_by in enumerate(OFFSETS):
        rows = sent_rows(tiles_ref, position, patches, column, shift_by, tile_count)
        for slot, first in enumerate(rows):
            packed_refs[column][slot] = features_ref[pl.ds(first, TILE), :]


def front_kernel(
    features_ref,
    cotangent_ref,
    weight_qkv_ref,
    weight_out_ref,
    normed_ref,
    normed_t_ref,
    cotangent_t_ref,
    projected_ref,
    grad_ref,
):
    normed = normalise(features_ref[...])[0].astype(jnp.bfloat16)
    normed_ref[...] = normed
    normed_t_ref[...] = normed.T
    cotangent_t_ref[...] = cotangent_ref[...].T
    projected_ref[...] = nn(normed, weight_qkv_ref[...]).astype(jnp.bfloat16)
    grad_ref[...] = nt(cotangent_ref[...], weight_out_ref[...]).astype(jnp.bfloat16)


def main_kernel(
    tiles_ref,
    valid_ref,
    place_ref,
    projected_ref,
    grad_ref,
    normed_ref,
    normed_t_ref,
    cotangent_t_ref,
    halo_a,
    halo_b,
    halo_c,
    halo_d,
    weight_ref,
    back_a,
    back_b,
    back_c,
    back_d,
    dquery_ref,
    dpair_ref,
    sent_ref,
    kept_ref,
    normed_s,
    pair_s,
    score_s,
    dprob_s,
    low_s,
    dscore_s,
    dkey_s,
    dvalue_s,
    dpair_s,
    attended_s,
):
    halos = (halo_a, halo_b, halo_c, halo_d)
    backs = (back_a, back_b, back_c, back_d)
    position = place_ref[0]
    rows_local, width = grad_ref.shape
    tile_count = rows_local // TILE
    head_width = width // HEADS
    scaling = head_width ** (-0.5)
    first_row = position * tile_count
    normed_s[:rows_local, :] = normed_ref[...]
    for column, halo in enumerate(halos):
        for slot in range(CAP):
            normed = normalise(halo[slot])[0].astype(jnp.bfloat16)
            first = rows_local + (column * CAP + slot) * TILE
            normed_s[first : first + TILE, :] = normed

    lane_tile = lax.broadcasted_iota(jnp.int32, (1, TILE), 1) * 0
    biases = []
    slots = []
    for tile in range(tile_count):
        row = first_row + tile
        pieces = []
        for other in range(tile_count):
            flag = jnp.int32(0)
            for column in range(LOCAL):
                flag = flag + jnp.where(
                    tiles_ref[row, column] == first_row + other, valid_ref[row, column], 0
                )
            pieces.append(jnp.where(lane_tile + flag > 0, 0.0, MASKED))
        places = []
        for column in range(len(OFFSETS)):
            high = named_pair(tiles_ref, first_row, LOCAL + column, tile_count)[1]
            place = jnp.where(tiles_ref[row, LOCAL + column] == high, 1, 0)
            places.append(column * CAP + place)
            flag = valid_ref[row, LOCAL + column]
            pieces.append(jnp.where(lane_tile + flag > 0, 0.0, MASKED))
        biases.append(jnp.concatenate(pieces, 1))
        slots.append(places)

    def one_head(head, carry):
        lanes = pl.ds(pl.multiple_of(head * head_width, head_width), head_width)
        key_lanes = pl.ds(pl.multiple_of(width + head * head_width, head_width), head_width)
        value_lanes = pl.ds(pl.multiple_of(2 * width + head * head_width, head_width), head_width)
        both = jnp.concatenate([weight_ref[:, key_lanes], weight_ref[:, value_lanes]], 1)
        pair_s[...] = nn(normed_s[rows_local:, :], both).astype(jnp.bfloat16)
        keys = projected_ref[:, key_lanes]
        values = projected_ref[:, value_lanes]
        score_s[:, :rows_local] = nt(projected_ref[:, lanes], keys)
        dprob_s[:, :rows_local] = nt(grad_ref[:, lanes], values)
        queries_t = projected_ref[:, lanes].T
        grads_t = grad_ref[:, lanes].T
        dkey_s[...] = jnp.zeros_like(dkey_s)
        dvalue_s[...] = jnp.zeros_like(dvalue_s)

        def rows_of(tile):
            return slice(tile * TILE, (tile + 1) * TILE)

        def halo_of(tile, part):
            starts = [pl.multiple_of(place * TILE, TILE) for place in slots[tile]]
            return jnp.concatenate([pair_s[pl.ds(start, TILE), part] for start in starts], 0)

        key_part, value_part = slice(0, head_width), slice(head_width, 2 * head_width)

        def products(tile):
            rows = rows_of(tile)
            score_s[rows, rows_local:] = nt(projected_ref[rows, lanes], halo_of(tile, key_part))
            dprob_s[rows, rows_local:] = nt(grad_ref[rows, lanes], halo_of(tile, value_part))

        def softmax(tile):
            chunks = [
                slice(first, first + CHUNK) for first in range(tile * TILE, (tile + 1) * TILE, CHUNK)
            ]
            highest = [
                jnp.max(score_s[chunk, :] * scaling + biases[tile], -1, keepdims=True)
                for chunk in chunks
            ]
            stats = []
            for chunk, high in zip(chunks, highest):
                expanded = jnp.exp(score_s[chunk, :] * scaling + (biases[tile] - high))
                score_s[chunk, :] = expanded
                over = 1.0 / jnp.sum(expanded, -1, keepdims=True)
                centre = jnp.sum(expanded * dprob_s[chunk, :], -1, keepdims=True) * over
                stats.append((over, centre))
            for chunk, (over, centre) in zip(chunks, stats):
                attention = score_s[chunk, :] * over
                low_s[chunk, :] = attention.astype(jnp.bfloat16)
                dscore = attention * (dprob_s[chunk, :] - centre)
                dscore_s[chunk, :] = dscore.astype(jnp.bfloat16)

        def finish(tile):
            rows = rows_of(tile)
            attended = nn(low_s[rows, :], jnp.concatenate([values, halo_of(tile, value_part)], 0))
            attended_s[rows, lanes] = attended.astype(jnp.bfloat16)
            key_all = jnp.concatenate([keys, halo_of(tile, key_part)], 0)
            dquery = nn(dscore_s[rows, :], key_all) * scaling
            dquery_ref[rows, lanes] = dquery.astype(jnp.bfloat16)
            dkey_t = nn(queries_t[:, rows], dscore_s[rows, rows_local:])
            dvalue_t = nn(grads_t[:, rows], low_s[rows, rows_local:])
            for column, place in enumerate(slots[tile]):
                part = slice(column * TILE, (column + 1) * TILE)
                dkey_s[place] += dkey_t[:, part]
                dvalue_s[place] += dvalue_t[:, part]

        products(0)
        for tile in range(tile_count):
            if tile + 1 < tile_count:
                products(tile + 1)
            if tile > 0:
                finish(tile - 1)
            softmax(tile)
        finish(tile_count - 1)
        low = jnp.bfloat16
        key_rows = lanes
        value_rows = key_lanes
        dpair_s[key_rows, :rows_local] = (nn(queries_t, dscore_s[:, :rows_local]) * scaling).astype(low)
        dpair_s[value_rows, :rows_local] = nn(grads_t, low_s[:, :rows_local]).astype(low)
        for place in range(SLOTS):
            part = slice(rows_local + place * TILE, rows_local + (place + 1) * TILE)
            dpair_s[key_rows, part] = (dkey_s[place] * scaling).astype(low)
            dpair_s[value_rows, part] = dvalue_s[place].astype(low)
        return carry

    lax.fori_loop(0, HEADS, one_head, 0)
    blocks = width // TILE
    side = place_ref[1]
    for out_ref, half in ((sent_ref, 1 - side), (kept_ref, side)):
        first = pl.multiple_of(half * width, width)
        pairs = nn(dpair_s[pl.ds(first, width), :], normed_s[...])
        store_blocks(out_ref, 0, pairs, blocks)

        @pl.when(half == 0)
        def _():
            store_blocks(out_ref, TILE, nn(normed_t_ref[...], dquery_ref[...]), blocks)

        @pl.when(half != 0)
        def _():
            store_blocks(out_ref, TILE, nn(cotangent_t_ref[...], attended_s[...]), blocks, True)

    for column, back in enumerate(backs):
        first = rows_local + column * CAP * TILE
        part = nn(weight_ref[:, width:], dpair_s[:, first : first + CAP * TILE])
        back[...] = part.astype(jnp.bfloat16).T.reshape(back.shape)
    dpair_ref[...] = dpair_s[:, :rows_local]


def store_blocks(out_ref, first, value, blocks, across=False):
    for row in range(blocks):
        for column in range(blocks):
            block = value[row * TILE : (row + 1) * TILE, column * TILE : (column + 1) * TILE]
            place = column * blocks + row if across else row * blocks + column
            start = place * 2 * TILE + first
            out_ref[start : start + TILE, :] = block.astype(out_ref.dtype)


def output_kernel(flip, place_ref, gathered_ref, *refs):
    qkv_ref, out_ref, pair_s, other_s, sems = refs[-5:]
    width = out_ref.shape[0]
    blocks = width // TILE
    half = place_ref[1] ^ flip
    first = pl.multiple_of((half + 1) * width, width)

    def spot(index):
        return slice(index * TILE, (index + 1) * TILE)

    def strips(row):
        start = pl.multiple_of(first + row * TILE, TILE)
        pair = pltpu.make_async_copy(
            pair_s.at[row], qkv_ref.at[:, pl.ds(start, TILE)], sems.at[row]
        )
        own, sem = other_s.at[row], sems.at[blocks + row]
        left = pltpu.make_async_copy(own, qkv_ref.at[spot(row), :width], sem)
        right = pltpu.make_async_copy(own, out_ref.at[spot(row), :], sem)
        return pair, left, right

    for row in range(blocks):
        pair, left, right = strips(row)
        for column in range(blocks):
            chunk = 2 * (row * blocks + column)
            pair_s[row, spot(column), :] = gathered_ref[spot(chunk), :].astype(jnp.float32)
            other_s[row, :, spot(column)] = gathered_ref[spot(chunk + 1), :].astype(jnp.float32)
        pair.start()
        pl.when(half == 0)(left.start)
        pl.when(half != 0)(right.start)
    for row in range(blocks):
        pair, left, right = strips(row)
        pair.wait()
        pl.when(half == 0)(left.wait)
        pl.when(half != 0)(right.wait)


def input_kernel(
    patches,
    tiles_ref,
    place_ref,
    features_ref,
    cotangent_ref,
    dquery_ref,
    dpair_ref,
    weight_ref,
    back_a,
    back_b,
    back_c,
    back_d,
    out_ref,
    total_s,
):
    position = place_ref[0]
    width = features_ref.shape[1]
    tile_count = features_ref.shape[0] // TILE
    pairs = nn(weight_ref[:, width:], dpair_ref[...])
    total_s[...] = nt(dquery_ref[...], weight_ref[:, :width]) + pairs.T
    for column, (shift_by, back) in enumerate(zip(OFFSETS, (back_a, back_b, back_c, back_d))):
        rows = sent_rows(tiles_ref, position, patches, column, shift_by, tile_count)
        for slot, first in enumerate(rows):
            total_s[pl.ds(first, TILE), :] += back[slot].astype(jnp.float32)
    normed, inverse = normalise(features_ref[...])
    total = total_s[...]
    centred = total - normed * jnp.mean(total * normed, -1, keepdims=True)
    out_ref[...] = (cotangent_ref[...].astype(jnp.float32) + inverse * centred).astype(out_ref.dtype)


def from_behind(value, steps):
    count = lax.axis_size("patch")
    pairs = [(source, (source + steps) % count) for source in range(count)]
    return lax.ppermute(value, "patch", pairs)


def exchange(value, flip, count):
    return lax.ppermute(value, AXES, [(source, source ^ flip) for source in range(count)])


def flips_of(bits):
    return [
        sum(((step >> place) & 1) << bit for place, bit in enumerate(bits))
        for step in range(1 << len(bits))
    ]


def digit_of(index, bits):
    return sum(((index >> bit) & 1) << place for place, bit in enumerate(bits))


def reduce_phase(value, index, bits, count):
    flips = flips_of(bits)
    digit = digit_of(index, bits)
    pieces = value.reshape(len(flips), value.shape[0] // len(flips), value.shape[1])
    received = [
        exchange(lax.dynamic_index_in_dim(pieces, digit ^ step, 0, False), flips[step], count)
        for step in range(1, len(flips))
    ]
    total = lax.dynamic_index_in_dim(pieces, digit, 0, False).astype(jnp.float32)
    for piece in received:
        total = total + piece.astype(jnp.float32)
    return total


def gather_phase(value, index, bits, count):
    flips = flips_of(bits)
    digit = digit_of(index, bits)
    pieces = [value]
    for flip in flips[1:]:
        pieces.append(exchange(value, flip, count))
    stacked = jnp.zeros((len(flips),) + value.shape, value.dtype)
    for step, piece in enumerate(pieces):
        stacked = lax.dynamic_update_index_in_dim(stacked, piece, digit ^ step, 0)
    return stacked.reshape(len(flips) * value.shape[0], value.shape[1])


def first_chunk(index, phases, chunks):
    spread, start = chunks, 0
    for bits in [[0]] + phases:
        spread = spread >> len(bits)
        start = start + digit_of(index, bits) * spread
    return start


def turned(value, first, chunks):
    pairs = value.reshape(-1, 2, TILE, TILE)
    flipped = jnp.swapaxes(pairs, 2, 3)
    chunk = first + jnp.arange(pairs.shape[0], dtype=jnp.int32)
    second = jnp.where((chunk < chunks // 2)[:, None, None], pairs[:, 1], flipped[:, 1])
    return jnp.stack([flipped[:, 0], second], 1).reshape(value.shape)


def on_device(features, cotangent, weight_qkv, weight_out, key_tiles, tile_valid):
    patches = lax.axis_size("patch")
    samples = lax.axis_size("sample")
    count = patches * samples
    position = lax.axis_index("patch").astype(jnp.int32)
    index = position * samples + lax.axis_index("sample").astype(jnp.int32)
    rows_local, width = features.shape[1:]
    rows = features[0]
    grad_rows = cotangent[0]
    low = jnp.bfloat16

    def shape(*dims, kind=low):
        return jax.ShapeDtypeStruct(dims, kind)

    def params(mebibytes):
        return pltpu.CompilerParams(vmem_limit_bytes=mebibytes << 20)

    place = jnp.stack([position, index & 1])
    packed = pl.pallas_call(
        partial(pack_kernel, patches),
        out_shape=[shape(CAP, TILE, width)] * len(OFFSETS),
        in_specs=[SMEM, SMEM, VMEM],
        out_specs=[VMEM] * len(OFFSETS),
        compiler_params=params(60),
        name="pack",
    )(key_tiles, place, rows)
    halos = [from_behind(piece, -shift_by) for piece, shift_by in zip(packed, OFFSETS)]
    square = shape(rows_local, width)
    normed_low, normed_t, cotangent_t, projected, grad_attended = pl.pallas_call(
        front_kernel,
        out_shape=[
            square,
            shape(width, rows_local),
            shape(width, rows_local),
            shape(rows_local, 3 * width),
            square,
        ],
        in_specs=[VMEM] * 4,
        out_specs=[VMEM] * 5,
        compiler_params=params(60),
        cost_estimate=pl.CostEstimate(
            flops=8 * rows_local * width * width, bytes_accessed=6 << 20, transcendentals=0
        ),
        name="front",
    )(rows, grad_rows, weight_qkv, weight_out)
    halo_rows = SLOTS * TILE
    all_rows = rows_local + halo_rows
    keys_seen = rows_local + len(OFFSETS) * TILE
    head_width = width // HEADS
    side = index & 1
    block_rows = 4 * width * width // TILE
    outs = pl.pallas_call(
        main_kernel,
        out_shape=[shape(CAP, TILE, width)] * len(OFFSETS)
        + [
            square,
            shape(2 * width, rows_local),
            shape(block_rows // 2, TILE),
            shape(block_rows // 2, TILE),
        ],
        in_specs=[SMEM] * 3 + [VMEM] * 10,
        out_specs=[VMEM] * (len(OFFSETS) + 4),
        scratch_shapes=[
            pltpu.VMEM((all_rows, width), low),
            pltpu.VMEM((halo_rows, 2 * head_width), low),
            pltpu.VMEM((rows_local, keys_seen), jnp.float32),
            pltpu.VMEM((rows_local, keys_seen), jnp.float32),
            pltpu.VMEM((rows_local, keys_seen), low),
            pltpu.VMEM((rows_local, keys_seen), low),
            pltpu.VMEM((SLOTS, head_width, TILE), jnp.float32),
            pltpu.VMEM((SLOTS, head_width, TILE), jnp.float32),
            pltpu.VMEM((2 * width, all_rows), low),
            pltpu.VMEM((rows_local, width), low),
        ],
        compiler_params=params(60),
        name="attend",
    )(
        key_tiles,
        tile_valid,
        place,
        projected,
        grad_attended,
        normed_low,
        normed_t,
        cotangent_t,
        *halos,
        weight_qkv,
    )
    backs, (dquery, dpair, sent, kept) = outs[:4], outs[4:]
    far = [column for column, shift_by in enumerate(OFFSETS) if abs(shift_by) == REACH]
    near = [column for column in range(len(OFFSETS)) if column not in far]
    backs = list(backs)
    returned = {}
    for column in far:
        returned[column] = from_behind(backs[column], OFFSETS[column])
    arrived = exchange(sent, 1, count)
    total = kept.astype(jnp.float32) + arrived.astype(jnp.float32)
    bit_count = count.bit_length() - 1
    phases = [list(range(bit, min(bit + 2, bit_count))) for bit in range(1, bit_count, 2)]
    for turn, bits in enumerate(phases):
        total = reduce_phase(total.astype(low), index, bits, count)
        if turn == 0:
            total, waiting = lax.optimization_barrier((total, [backs[column] for column in near]))
            for column, piece in zip(near, waiting):
                returned[column] = from_behind(piece, OFFSETS[column])
    factor = float(count * rows_local) ** (-0.5)
    total = total * factor
    chunks = block_rows // (2 * TILE)
    whole_chunks = total.shape[0] % (2 * TILE) == 0
    if whole_chunks:
        total = turned(total, first_chunk(index, phases, chunks), chunks)
    gathered = total.astype(low)
    grad_features = None
    for turn, bits in enumerate(phases[::-1]):
        if turn == 1:
            gathered, held = lax.optimization_barrier(
                (gathered, [returned[column] for column in range(len(OFFSETS))])
            )
            grad_features = pl.pallas_call(
                partial(input_kernel, patches),
                out_shape=square,
                in_specs=[SMEM, SMEM] + [VMEM] * 9,
                out_specs=VMEM,
                scratch_shapes=[pltpu.VMEM((rows_local, width), jnp.float32)],
                compiler_params=params(60),
                cost_estimate=pl.CostEstimate(
                    flops=6 * rows_local * width * width, bytes_accessed=6 << 20, transcendentals=0
                ),
                name="inputs",
            )(key_tiles, place, rows, grad_rows, dquery, dpair, weight_qkv, *held)
        gathered = gather_phase(gathered, index, bits, count)
    other = exchange(gathered, 1, count)
    if not whole_chunks:
        gathered = turned(gathered, side * (chunks // 2), chunks)
        other = turned(other, (1 - side) * (chunks // 2), chunks)

    def outputs(flip, half, *started):
        return pl.pallas_call(
            partial(output_kernel, flip),
            out_shape=[
                shape(width, 3 * width, kind=jnp.float32),
                shape(width, width, kind=jnp.float32),
            ],
            in_specs=[SMEM, VMEM] + [ANY] * len(started),
            out_specs=[ANY] * 2,
            scratch_shapes=[
                pltpu.VMEM((width // TILE, width, TILE), jnp.float32),
                pltpu.VMEM((width // TILE, TILE, width), jnp.float32),
                pltpu.SemaphoreType.DMA((2 * width // TILE,)),
            ],
            input_output_aliases={2: 0, 3: 1} if started else {},
            compiler_params=params(10),
            cost_estimate=pl.CostEstimate(flops=0, bytes_accessed=4 << 20, transcendentals=0),
            name="outputs",
        )(place, half, *started)

    started = outputs(0, gathered)
    grad_qkv, grad_out = outputs(1, other, *started)
    return (grad_features[None], grad_qkv, grad_out)


def solution(mesh):
    placed = (P("sample", "patch", None), P("sample", "patch", None), P(), P(), P(), P())
    return jax.shard_map(
        on_device,
        mesh=mesh,
        in_specs=placed,
        out_specs=(P("sample", "patch", None), P(), P()),
        check_vma=False,
    )
```

```python
from functools import partial
import math

import jax
import jax.numpy as jnp
from jax import lax
from jax.experimental import pallas as pl
from jax.experimental.pallas import tpu as pltpu
from jax.sharding import PartitionSpec as P


HEADS = 4
TILE = 128
NB = 8
REACH = 2
CAP = 2
OFFSETS = [shift_by for shift_by in range(-REACH, REACH + 1) if shift_by != 0]
LOCAL = NB - len(OFFSETS)
SLOTS = CAP * len(OFFSETS)
MASKED = -1e30
CHUNK = 16
OPEN_AT = 3
AXES = ("patch", "sample")

epsilon = 1e-06

VMEM = pl.BlockSpec(memory_space=pltpu.VMEM)
SMEM = pl.BlockSpec(memory_space=pltpu.SMEM)
ANY = pl.BlockSpec(memory_space=pl.ANY)


def nn(a, b):
    return jnp.dot(a, b, preferred_element_type=jnp.float32)


def nt(a, b):
    return lax.dot_general(a, b, (((1,), (1,)), ((), ())), preferred_element_type=jnp.float32)


def normalise(rows):
    inputs = rows.astype(jnp.float32)
    inverse = lax.rsqrt(jnp.mean(inputs * inputs, -1, keepdims=True) + epsilon)
    return inputs * inverse, inverse


def named_pair(tiles_ref, first_row, column, count):
    named = [tiles_ref[first_row + row, column] for row in range(count)]
    low = high = named[0]
    for entry in named[1:]:
        low = jnp.minimum(low, entry)
        high = jnp.maximum(high, entry)
    return low, high


def sent_rows(tiles_ref, position, patches, column, shift_by, tile_count):
    target = lax.rem(position - shift_by + patches, patches)
    pair = named_pair(tiles_ref, target * tile_count, LOCAL + column, tile_count)
    return [pl.multiple_of((entry - position * tile_count) * TILE, TILE) for entry in pair]


def pack_kernel(patches, tiles_ref, place_ref, features_ref, *packed_refs):
    position = place_ref[0]
    tile_count = features_ref.shape[0] // TILE
    for column, shift_by in enumerate(OFFSETS):
        rows = sent_rows(tiles_ref, position, patches, column, shift_by, tile_count)
        for slot, first in enumerate(rows):
            packed_refs[column][slot] = features_ref[pl.ds(first, TILE), :]


def front_kernel(
    features_ref,
    cotangent_ref,
    weight_qkv_ref,
    weight_out_ref,
    normed_ref,
    normed_t_ref,
    cotangent_t_ref,
    projected_ref,
    grad_ref,
):
    normed = normalise(features_ref[...])[0].astype(jnp.bfloat16)
    normed_ref[...] = normed
    normed_t_ref[...] = normed.T
    cotangent_t_ref[...] = cotangent_ref[...].T
    projected_ref[...] = nn(normed, weight_qkv_ref[...]).astype(jnp.bfloat16)
    grad_ref[...] = nt(cotangent_ref[...], weight_out_ref[...]).astype(jnp.bfloat16)


def main_kernel(
    tiles_ref,
    valid_ref,
    place_ref,
    projected_ref,
    grad_ref,
    normed_ref,
    normed_t_ref,
    cotangent_t_ref,
    halo_a,
    halo_b,
    halo_c,
    halo_d,
    weight_ref,
    back_a,
    back_b,
    back_c,
    back_d,
    dquery_ref,
    dpair_ref,
    sent_ref,
    kept_ref,
    normed_s,
    pair_s,
    score_s,
    dprob_s,
    low_s,
    dscore_s,
    dkey_s,
    dvalue_s,
    dpair_s,
    attended_s,
    turned_s,
):
    halos = (halo_a, halo_b, halo_c, halo_d)
    backs = (back_a, back_b, back_c, back_d)
    position = place_ref[0]
    rows_local, width = grad_ref.shape
    tile_count = rows_local // TILE
    head_width = width // HEADS
    scaling = head_width ** (-0.5)
    scaling_2 = scaling * math.log2(math.e)
    first_row = position * tile_count
    normed_s[:rows_local, :] = normed_ref[...]
    for column, halo in enumerate(halos):
        for slot in range(CAP):
            normed = normalise(halo[slot])[0].astype(jnp.bfloat16)
            first = rows_local + (column * CAP + slot) * TILE
            normed_s[first : first + TILE, :] = normed

    lane_tile = lax.broadcasted_iota(jnp.int32, (1, TILE), 1) * 0
    biases = []
    slots = []
    for tile in range(tile_count):
        row = first_row + tile
        pieces = []
        for other in range(tile_count):
            flag = jnp.int32(0)
            for column in range(LOCAL):
                flag = flag + jnp.where(
                    tiles_ref[row, column] == first_row + other, valid_ref[row, column], 0
                )
            pieces.append(jnp.where(lane_tile + flag > 0, 0.0, MASKED))
        places = []
        for column in range(len(OFFSETS)):
            high = named_pair(tiles_ref, first_row, LOCAL + column, tile_count)[1]
            place = jnp.where(tiles_ref[row, LOCAL + column] == high, 1, 0)
            places.append(column * CAP + place)
            flag = valid_ref[row, LOCAL + column]
            pieces.append(jnp.where(lane_tile + flag > 0, 0.0, MASKED))
        biases.append(jnp.concatenate(pieces, 1))
        slots.append(places)

    low = jnp.bfloat16
    key_part, value_part = slice(0, head_width), slice(head_width, 2 * head_width)

    def lanes_of(part, head):
        return pl.ds(part * width + head * head_width, head_width)

    def rows_of(tile):
        return slice(tile * TILE, (tile + 1) * TILE)

    def halo_of(head, tile, part):
        starts = [pl.multiple_of(place * TILE, TILE) for place in slots[tile]]
        return jnp.concatenate([pair_s[head % 2, pl.ds(start, TILE), part] for start in starts], 0)

    def project(head):
        both = jnp.concatenate(
            [weight_ref[:, lanes_of(1, head)], weight_ref[:, lanes_of(2, head)]], 1
        )
        pair_s[head % 2] = nn(normed_s[rows_local:, :], both).astype(low)

    def open_head(head):
        turn = head % 2
        lanes = lanes_of(0, head)
        local = nt(projected_ref[:, lanes], projected_ref[:, lanes_of(1, head)])
        for tile in range(tile_count):
            rows = rows_of(tile)
            score_s[turn, rows, :rows_local] = local[rows, :] + biases[tile][:, :rows_local]
        dprob_s[turn, :, :rows_local] = nt(grad_ref[:, lanes], projected_ref[:, lanes_of(2, head)])
        turned_s[turn, 0] = projected_ref[:, lanes].T
        turned_s[turn, 1] = grad_ref[:, lanes].T
        dkey_s[turn] = jnp.zeros(dkey_s.shape[1:], jnp.float32)
        dvalue_s[turn] = jnp.zeros(dvalue_s.shape[1:], jnp.float32)

    def products(head, tile):
        turn, rows, lanes = head % 2, rows_of(tile), lanes_of(0, head)
        seen = nt(projected_ref[rows, lanes], halo_of(head, tile, key_part))
        score_s[turn, rows, rows_local:] = seen + biases[tile][:, rows_local:]
        dprob_s[turn, rows, rows_local:] = nt(grad_ref[rows, lanes], halo_of(head, tile, value_part))

    def softmax(head, tile):
        turn = head % 2
        chunks = [
            slice(first, first + CHUNK) for first in range(tile * TILE, (tile + 1) * TILE, CHUNK)
        ]
        highest = [jnp.max(score_s[turn, chunk, :], -1, keepdims=True) for chunk in chunks]
        stats = []
        for chunk, high in zip(chunks, highest):
            expanded = jnp.exp2(score_s[turn, chunk, :] * scaling_2 - high * scaling_2)
            score_s[turn, chunk, :] = expanded
            over = 1.0 / jnp.sum(expanded, -1, keepdims=True)
            centre = jnp.sum(expanded * dprob_s[turn, chunk, :], -1, keepdims=True) * over
            stats.append((over, centre))
        for chunk, (over, centre) in zip(chunks, stats):
            attention = score_s[turn, chunk, :] * over
            low_s[turn, chunk, :] = attention.astype(low)
            dscore_s[turn, chunk, :] = (attention * (dprob_s[turn, chunk, :] - centre)).astype(low)

    def finish(head, tile):
        turn, rows, lanes = head % 2, rows_of(tile), lanes_of(0, head)
        values = projected_ref[:, lanes_of(2, head)]
        value_all = jnp.concatenate([values, halo_of(head, tile, value_part)], 0)
        attended_s[rows, lanes] = nn(low_s[turn, rows, :], value_all).astype(low)
        keys = projected_ref[:, lanes_of(1, head)]
        key_all = jnp.concatenate([keys, halo_of(head, tile, key_part)], 0)
        dquery_ref[rows, lanes] = (nn(dscore_s[turn, rows, :], key_all) * scaling).astype(low)
        dkey_t = nn(turned_s[turn, 0, :, rows], dscore_s[turn, rows, rows_local:])
        dvalue_t = nn(turned_s[turn, 1, :, rows], low_s[turn, rows, rows_local:])
        for column, place in enumerate(slots[tile]):
            part = slice(column * TILE, (column + 1) * TILE)
            dkey_s[turn, place] += dkey_t[:, part]
            dvalue_s[turn, place] += dvalue_t[:, part]

    def close_head(head):
        turn = head % 2
        key_rows, value_rows = lanes_of(0, head), lanes_of(1, head)
        dkey = nn(turned_s[turn, 0], dscore_s[turn, :, :rows_local]) * scaling
        dpair_s[key_rows, :rows_local] = dkey.astype(low)
        dpair_s[value_rows, :rows_local] = nn(turned_s[turn, 1], low_s[turn, :, :rows_local]).astype(low)
        for place in range(SLOTS):
            part = slice(rows_local + place * TILE, rows_local + (place + 1) * TILE)
            dpair_s[key_rows, part] = (dkey_s[turn, place] * scaling).astype(low)
            dpair_s[value_rows, part] = dvalue_s[turn, place].astype(low)

    steps = [(head, tile) for head in range(HEADS) for tile in range(tile_count)]
    project(0)
    open_head(0)
    products(*steps[0])
    for place, (head, tile) in enumerate(steps):
        if tile == 1 and head + 1 < HEADS:
            project(head + 1)
        if tile == OPEN_AT and head + 1 < HEADS:
            open_head(head + 1)
        if place + 1 < len(steps):
            products(*steps[place + 1])
        if place > 0:
            finish(*steps[place - 1])
            if tile == 0:
                close_head(head - 1)
        softmax(head, tile)
    finish(*steps[-1])
    close_head(HEADS - 1)
    blocks = width // TILE
    side = place_ref[1]
    for out_ref, half in ((sent_ref, 1 - side), (kept_ref, side)):
        first = pl.multiple_of(half * width, width)
        pairs = nn(dpair_s[pl.ds(first, width), :], normed_s[...])
        store_blocks(out_ref, 0, pairs, blocks)

        @pl.when(half == 0)
        def _():
            store_blocks(out_ref, TILE, nn(normed_t_ref[...], dquery_ref[...]), blocks)

        @pl.when(half != 0)
        def _():
            store_blocks(out_ref, TILE, nn(cotangent_t_ref[...], attended_s[...]), blocks, True)

    for column, back in enumerate(backs):
        first = rows_local + column * CAP * TILE
        part = nn(weight_ref[:, width:], dpair_s[:, first : first + CAP * TILE])
        back[...] = part.astype(jnp.bfloat16).T.reshape(back.shape)
    dpair_ref[...] = dpair_s[:, :rows_local]


def main_scratch(rows_local, width):
    halo_rows = SLOTS * TILE
    all_rows = rows_local + halo_rows
    keys_seen = rows_local + len(OFFSETS) * TILE
    head_width = width // HEADS
    low = jnp.bfloat16
    return [
        pltpu.VMEM((all_rows, width), low),
        pltpu.VMEM((2, halo_rows, 2 * head_width), low),
        pltpu.VMEM((2, rows_local, keys_seen), jnp.float32),
        pltpu.VMEM((2, rows_local, keys_seen), jnp.float32),
        pltpu.VMEM((2, rows_local, keys_seen), low),
        pltpu.VMEM((2, rows_local, keys_seen), low),
        pltpu.VMEM((2, SLOTS, head_width, TILE), jnp.float32),
        pltpu.VMEM((2, SLOTS, head_width, TILE), jnp.float32),
        pltpu.VMEM((2 * width, all_rows), low),
        pltpu.VMEM((rows_local, width), low),
        pltpu.VMEM((2, 2, head_width, rows_local), low),
    ]


def store_blocks(out_ref, first, value, blocks, across=False):
    for row in range(blocks):
        for column in range(blocks):
            block = value[row * TILE : (row + 1) * TILE, column * TILE : (column + 1) * TILE]
            place = column * blocks + row if across else row * blocks + column
            start = place * 2 * TILE + first
            out_ref[start : start + TILE, :] = block.astype(out_ref.dtype)


def output_kernel(flip, place_ref, gathered_ref, *refs):
    qkv_ref, out_ref, pair_s, other_s, sems = refs[-5:]
    width = out_ref.shape[0]
    blocks = width // TILE
    half = place_ref[1] ^ flip
    first = pl.multiple_of((half + 1) * width, width)

    def spot(index):
        return slice(index * TILE, (index + 1) * TILE)

    def strips(row):
        start = pl.multiple_of(first + row * TILE, TILE)
        pair = pltpu.make_async_copy(
            pair_s.at[row], qkv_ref.at[:, pl.ds(start, TILE)], sems.at[row]
        )
        own, sem = other_s.at[row], sems.at[blocks + row]
        left = pltpu.make_async_copy(own, qkv_ref.at[spot(row), :width], sem)
        right = pltpu.make_async_copy(own, out_ref.at[spot(row), :], sem)
        return pair, left, right

    for row in range(blocks):
        pair, left, right = strips(row)
        for column in range(blocks):
            chunk = 2 * (row * blocks + column)
            pair_s[row, spot(column), :] = gathered_ref[spot(chunk), :].astype(jnp.float32)
            other_s[row, :, spot(column)] = gathered_ref[spot(chunk + 1), :].astype(jnp.float32)
        pair.start()
        pl.when(half == 0)(left.start)
        pl.when(half != 0)(right.start)
    for row in range(blocks):
        pair, left, right = strips(row)
        pair.wait()
        pl.when(half == 0)(left.wait)
        pl.when(half != 0)(right.wait)


def input_kernel(
    patches,
    tiles_ref,
    place_ref,
    features_ref,
    cotangent_ref,
    dquery_ref,
    dpair_ref,
    weight_ref,
    back_a,
    back_b,
    back_c,
    back_d,
    out_ref,
    total_s,
):
    position = place_ref[0]
    width = features_ref.shape[1]
    tile_count = features_ref.shape[0] // TILE
    pairs = nn(weight_ref[:, width:], dpair_ref[...])
    total_s[...] = nt(dquery_ref[...], weight_ref[:, :width]) + pairs.T
    for column, (shift_by, back) in enumerate(zip(OFFSETS, (back_a, back_b, back_c, back_d))):
        rows = sent_rows(tiles_ref, position, patches, column, shift_by, tile_count)
        for slot, first in enumerate(rows):
            total_s[pl.ds(first, TILE), :] += back[slot].astype(jnp.float32)
    normed, inverse = normalise(features_ref[...])
    total = total_s[...]
    centred = total - normed * jnp.mean(total * normed, -1, keepdims=True)
    out_ref[...] = (cotangent_ref[...].astype(jnp.float32) + inverse * centred).astype(out_ref.dtype)


def from_behind(value, steps):
    count = lax.axis_size("patch")
    pairs = [(source, (source + steps) % count) for source in range(count)]
    return lax.ppermute(value, "patch", pairs)


def exchange(value, flip, count):
    return lax.ppermute(value, AXES, [(source, source ^ flip) for source in range(count)])


def flips_of(bits):
    return [
        sum(((step >> place) & 1) << bit for place, bit in enumerate(bits))
        for step in range(1 << len(bits))
    ]


def digit_of(index, bits):
    return sum(((index >> bit) & 1) << place for place, bit in enumerate(bits))


def reduce_phase(value, index, bits, count):
    flips = flips_of(bits)
    digit = digit_of(index, bits)
    pieces = value.reshape(len(flips), value.shape[0] // len(flips), value.shape[1])
    received = []
    for step in range(1, len(flips)):
        piece = lax.dynamic_index_in_dim(pieces, digit ^ step, 0, False)
        received.append(exchange(piece, flips[step], count))
    total = lax.dynamic_index_in_dim(pieces, digit, 0, False).astype(jnp.float32)
    for piece in received:
        total = total + piece.astype(jnp.float32)
    return total


def gather_phase(value, index, bits, count):
    flips = flips_of(bits)
    digit = digit_of(index, bits)
    pieces = [value]
    for flip in flips[1:]:
        pieces.append(exchange(value, flip, count))
    stacked = jnp.zeros((len(flips),) + value.shape, value.dtype)
    for step, piece in enumerate(pieces):
        stacked = lax.dynamic_update_index_in_dim(stacked, piece, digit ^ step, 0)
    return stacked.reshape(len(flips) * value.shape[0], value.shape[1])


def first_chunk(index, phases, chunks):
    spread, start = chunks, 0
    for bits in [[0]] + phases:
        spread = spread >> len(bits)
        start = start + digit_of(index, bits) * spread
    return start


def turned(value, first, chunks):
    pairs = value.reshape(-1, 2, TILE, TILE)
    flipped = jnp.swapaxes(pairs, 2, 3)
    chunk = first + jnp.arange(pairs.shape[0], dtype=jnp.int32)
    second = jnp.where((chunk < chunks // 2)[:, None, None], pairs[:, 1], flipped[:, 1])
    return jnp.stack([flipped[:, 0], second], 1).reshape(value.shape)


def on_device(features, cotangent, weight_qkv, weight_out, key_tiles, tile_valid):
    patches = lax.axis_size("patch")
    samples = lax.axis_size("sample")
    count = patches * samples
    position = lax.axis_index("patch").astype(jnp.int32)
    index = position * samples + lax.axis_index("sample").astype(jnp.int32)
    rows_local, width = features.shape[1:]
    rows = features[0]
    grad_rows = cotangent[0]
    low = jnp.bfloat16

    def shape(*dims, kind=low):
        return jax.ShapeDtypeStruct(dims, kind)

    def params(mebibytes):
        return pltpu.CompilerParams(vmem_limit_bytes=mebibytes << 20)

    place = jnp.stack([position, index & 1])
    packed = pl.pallas_call(
        partial(pack_kernel, patches),
        out_shape=[shape(CAP, TILE, width)] * len(OFFSETS),
        in_specs=[SMEM, SMEM, VMEM],
        out_specs=[VMEM] * len(OFFSETS),
        compiler_params=params(60),
        name="pack",
    )(key_tiles, place, rows)
    halos = [from_behind(piece, -shift_by) for piece, shift_by in zip(packed, OFFSETS)]
    square = shape(rows_local, width)
    normed_low, normed_t, cotangent_t, projected, grad_attended = pl.pallas_call(
        front_kernel,
        out_shape=[
            square,
            shape(width, rows_local),
            shape(width, rows_local),
            shape(rows_local, 3 * width),
            square,
        ],
        in_specs=[VMEM] * 4,
        out_specs=[VMEM] * 5,
        compiler_params=params(60),
        cost_estimate=pl.CostEstimate(
            flops=8 * rows_local * width * width, bytes_accessed=6 << 20, transcendentals=0
        ),
        name="front",
    )(rows, grad_rows, weight_qkv, weight_out)
    side = index & 1
    block_rows = 4 * width * width // TILE
    outs = pl.pallas_call(
        main_kernel,
        out_shape=[shape(CAP, TILE, width)] * len(OFFSETS)
        + [
            square,
            shape(2 * width, rows_local),
            shape(block_rows // 2, TILE),
            shape(block_rows // 2, TILE),
        ],
        in_specs=[SMEM] * 3 + [VMEM] * 10,
        out_specs=[VMEM] * (len(OFFSETS) + 4),
        scratch_shapes=main_scratch(rows_local, width),
        compiler_params=params(60),
        name="attend",
    )(
        key_tiles,
        tile_valid,
        place,
        projected,
        grad_attended,
        normed_low,
        normed_t,
        cotangent_t,
        *halos,
        weight_qkv,
    )
    backs, (dquery, dpair, sent, kept) = outs[:4], outs[4:]
    far = [column for column, shift_by in enumerate(OFFSETS) if abs(shift_by) == REACH]
    near = [column for column in range(len(OFFSETS)) if column not in far]
    backs = list(backs)
    returned = {}
    for column in far:
        returned[column] = from_behind(backs[column], OFFSETS[column])
    arrived = exchange(sent, 1, count)
    total = kept.astype(jnp.float32) + arrived.astype(jnp.float32)
    bit_count = count.bit_length() - 1
    phases = [list(range(bit, min(bit + 2, bit_count))) for bit in range(1, bit_count, 2)]
    for turn, bits in enumerate(phases):
        total = reduce_phase(total.astype(low), index, bits, count)
        if turn == 0:
            total, waiting = lax.optimization_barrier((total, [backs[column] for column in near]))
            for column, piece in zip(near, waiting):
                returned[column] = from_behind(piece, OFFSETS[column])
    factor = float(count * rows_local) ** (-0.5)
    total = total * factor
    chunks = block_rows // (2 * TILE)
    whole_chunks = total.shape[0] % (2 * TILE) == 0
    if whole_chunks:
        total = turned(total, first_chunk(index, phases, chunks), chunks)
    gathered = total.astype(low)
    grad_features = None
    for turn, bits in enumerate(phases[::-1]):
        if turn == 1:
            gathered, held = lax.optimization_barrier(
                (gathered, [returned[column] for column in range(len(OFFSETS))])
            )
            grad_features = pl.pallas_call(
                partial(input_kernel, patches),
                out_shape=square,
                in_specs=[SMEM, SMEM] + [VMEM] * 9,
                out_specs=VMEM,
                scratch_shapes=[pltpu.VMEM((rows_local, width), jnp.float32)],
                compiler_params=params(60),
                cost_estimate=pl.CostEstimate(
                    flops=6 * rows_local * width * width, bytes_accessed=6 << 20, transcendentals=0
                ),
                name="inputs",
            )(key_tiles, place, rows, grad_rows, dquery, dpair, weight_qkv, *held)
        gathered = gather_phase(gathered, index, bits, count)
    other = exchange(gathered, 1, count)
    if not whole_chunks:
        gathered = turned(gathered, side * (chunks // 2), chunks)
        other = turned(other, (1 - side) * (chunks // 2), chunks)

    def outputs(flip, half, *started):
        return pl.pallas_call(
            partial(output_kernel, flip),
            out_shape=[
                shape(width, 3 * width, kind=jnp.float32),
                shape(width, width, kind=jnp.float32),
            ],
            in_specs=[SMEM, VMEM] + [ANY] * len(started),
            out_specs=[ANY] * 2,
            scratch_shapes=[
                pltpu.VMEM((width // TILE, width, TILE), jnp.float32),
                pltpu.VMEM((width // TILE, TILE, width), jnp.float32),
                pltpu.SemaphoreType.DMA((2 * width // TILE,)),
            ],
            input_output_aliases={2: 0, 3: 1} if started else {},
            compiler_params=params(10),
            cost_estimate=pl.CostEstimate(flops=0, bytes_accessed=4 << 20, transcendentals=0),
            name="outputs",
        )(place, half, *started)

    started = outputs(0, gathered)
    grad_qkv, grad_out = outputs(1, other, *started)
    return (grad_features[None], grad_qkv, grad_out)


def solution(mesh):
    placed = (P("sample", "patch", None), P("sample", "patch", None), P(), P(), P(), P())
    return jax.shard_map(
        on_device,
        mesh=mesh,
        in_specs=placed,
        out_specs=(P("sample", "patch", None), P(), P()),
        check_vma=False,
    )
```

```python
from functools import partial
import math

import jax
import jax.numpy as jnp
from jax import lax
from jax.experimental import pallas as pl
from jax.experimental.pallas import tpu as pltpu
from jax.sharding import PartitionSpec as P


HEADS = 4
TILE = 128
NB = 8
REACH = 2
CAP = 2
OFFSETS = [shift_by for shift_by in range(-REACH, REACH + 1) if shift_by != 0]
LOCAL = NB - len(OFFSETS)
SLOTS = CAP * len(OFFSETS)
MASKED = -1e30
CHUNK = 16
OPEN_AT = 3
AXES = ("patch", "sample")

epsilon = 1e-06

VMEM = pl.BlockSpec(memory_space=pltpu.VMEM)
SMEM = pl.BlockSpec(memory_space=pltpu.SMEM)
ANY = pl.BlockSpec(memory_space=pl.ANY)


def nn(a, b):
    return jnp.dot(a, b, preferred_element_type=jnp.float32)


def nt(a, b):
    return lax.dot_general(a, b, (((1,), (1,)), ((), ())), preferred_element_type=jnp.float32)


def normalise(rows):
    inputs = rows.astype(jnp.float32)
    inverse = lax.rsqrt(jnp.mean(inputs * inputs, -1, keepdims=True) + epsilon)
    return inputs * inverse, inverse


def named_pair(tiles_ref, first_row, column, count):
    named = [tiles_ref[column, first_row + row] for row in range(count)]
    low = high = named[0]
    for entry in named[1:]:
        low = jnp.minimum(low, entry)
        high = jnp.maximum(high, entry)
    return low, high


def sent_rows(tiles_ref, position, patches, column, shift_by, tile_count):
    target = lax.rem(position - shift_by + patches, patches)
    pair = named_pair(tiles_ref, target * tile_count, LOCAL + column, tile_count)
    return [pl.multiple_of((entry - position * tile_count) * TILE, TILE) for entry in pair]


def pack_kernel(patches, tiles_ref, features_ref, *packed_refs):
    position = lax.axis_index("patch").astype(jnp.int32)
    tile_count = features_ref.shape[0] // TILE
    for column, shift_by in enumerate(OFFSETS):
        rows = sent_rows(tiles_ref, position, patches, column, shift_by, tile_count)
        for slot, first in enumerate(rows):
            packed_refs[column][slot] = features_ref[pl.ds(first, TILE), :]


def front_kernel(
    features_ref,
    cotangent_ref,
    weight_qkv_ref,
    weight_out_ref,
    normed_ref,
    normed_t_ref,
    cotangent_t_ref,
    projected_ref,
    grad_ref,
):
    normed = normalise(features_ref[...])[0].astype(jnp.bfloat16)
    normed_ref[...] = normed
    normed_t_ref[...] = normed.T
    cotangent_t_ref[...] = cotangent_ref[...].T
    projected_ref[...] = nn(normed, weight_qkv_ref[...]).astype(jnp.bfloat16)
    grad_ref[...] = nt(cotangent_ref[...], weight_out_ref[...]).astype(jnp.bfloat16)


def main_kernel(
    tiles_ref,
    valid_ref,
    place_ref,
    projected_ref,
    grad_ref,
    normed_ref,
    normed_t_ref,
    cotangent_t_ref,
    halo_a,
    halo_b,
    halo_c,
    halo_d,
    weight_ref,
    back_a,
    back_b,
    back_c,
    back_d,
    dquery_ref,
    dpair_ref,
    sent_ref,
    kept_ref,
    normed_s,
    pair_s,
    score_s,
    dprob_s,
    low_s,
    dscore_s,
    dkey_s,
    dvalue_s,
    dpair_s,
    attended_s,
    turned_s,
):
    halos = (halo_a, halo_b, halo_c, halo_d)
    backs = (back_a, back_b, back_c, back_d)
    position = place_ref[0]
    rows_local, width = grad_ref.shape
    tile_count = rows_local // TILE
    head_width = width // HEADS
    scaling = head_width ** (-0.5)
    scaling_2 = scaling * math.log2(math.e)
    first_row = position * tile_count
    normed_s[:rows_local, :] = normed_ref[...]
    for column, halo in enumerate(halos):
        for slot in range(CAP):
            normed = normalise(halo[slot])[0].astype(jnp.bfloat16)
            first = rows_local + (column * CAP + slot) * TILE
            normed_s[first : first + TILE, :] = normed

    lane_tile = lax.broadcasted_iota(jnp.int32, (1, TILE), 1) * 0
    biases = []
    slots = []
    for tile in range(tile_count):
        row = first_row + tile
        pieces = []
        for other in range(tile_count):
            flag = jnp.int32(0)
            for column in range(LOCAL):
                flag = flag + jnp.where(
                    tiles_ref[column, row] == first_row + other, valid_ref[column, row], 0
                )
            pieces.append(jnp.where(lane_tile + flag > 0, 0.0, MASKED))
        places = []
        for column in range(len(OFFSETS)):
            high = named_pair(tiles_ref, first_row, LOCAL + column, tile_count)[1]
            place = jnp.where(tiles_ref[LOCAL + column, row] == high, 1, 0)
            places.append(column * CAP + place)
            flag = valid_ref[LOCAL + column, row]
            pieces.append(jnp.where(lane_tile + flag > 0, 0.0, MASKED))
        biases.append(jnp.concatenate(pieces, 1))
        slots.append(places)

    low = jnp.bfloat16
    key_part, value_part = slice(0, head_width), slice(head_width, 2 * head_width)

    def lanes_of(part, head):
        return pl.ds(part * width + head * head_width, head_width)

    def rows_of(tile):
        return slice(tile * TILE, (tile + 1) * TILE)

    def halo_of(head, tile, part):
        starts = [pl.multiple_of(place * TILE, TILE) for place in slots[tile]]
        return jnp.concatenate([pair_s[head % 2, pl.ds(start, TILE), part] for start in starts], 0)

    def project(head):
        both = jnp.concatenate(
            [weight_ref[:, lanes_of(1, head)], weight_ref[:, lanes_of(2, head)]], 1
        )
        pair_s[head % 2] = nn(normed_s[rows_local:, :], both).astype(low)

    def open_head(head):
        turn = head % 2
        lanes = lanes_of(0, head)
        local = nt(projected_ref[:, lanes], projected_ref[:, lanes_of(1, head)])
        for tile in range(tile_count):
            rows = rows_of(tile)
            score_s[turn, rows, :rows_local] = local[rows, :] + biases[tile][:, :rows_local]
        dprob_s[turn, :, :rows_local] = nt(grad_ref[:, lanes], projected_ref[:, lanes_of(2, head)])
        turned_s[turn, 0] = projected_ref[:, lanes].T
        turned_s[turn, 1] = grad_ref[:, lanes].T
        dkey_s[turn] = jnp.zeros(dkey_s.shape[1:], jnp.float32)
        dvalue_s[turn] = jnp.zeros(dvalue_s.shape[1:], jnp.float32)

    def products(head, tile):
        turn, rows, lanes = head % 2, rows_of(tile), lanes_of(0, head)
        seen = nt(projected_ref[rows, lanes], halo_of(head, tile, key_part))
        score_s[turn, rows, rows_local:] = seen + biases[tile][:, rows_local:]
        dprob_s[turn, rows, rows_local:] = nt(grad_ref[rows, lanes], halo_of(head, tile, value_part))

    def softmax(head, tile):
        turn = head % 2
        chunks = [
            slice(first, first + CHUNK) for first in range(tile * TILE, (tile + 1) * TILE, CHUNK)
        ]
        highest = [jnp.max(score_s[turn, chunk, :], -1, keepdims=True) for chunk in chunks]
        stats = []
        for chunk, high in zip(chunks, highest):
            expanded = jnp.exp2(score_s[turn, chunk, :] * scaling_2 - high * scaling_2)
            score_s[turn, chunk, :] = expanded
            over = 1.0 / jnp.sum(expanded, -1, keepdims=True)
            centre = jnp.sum(expanded * dprob_s[turn, chunk, :], -1, keepdims=True) * over
            stats.append((over, centre))
        for chunk, (over, centre) in zip(chunks, stats):
            attention = score_s[turn, chunk, :] * over
            low_s[turn, chunk, :] = attention.astype(low)
            dscore_s[turn, chunk, :] = (attention * (dprob_s[turn, chunk, :] - centre)).astype(low)

    def finish(head, tile):
        turn, rows, lanes = head % 2, rows_of(tile), lanes_of(0, head)
        values = projected_ref[:, lanes_of(2, head)]
        value_all = jnp.concatenate([values, halo_of(head, tile, value_part)], 0)
        attended_s[rows, lanes] = nn(low_s[turn, rows, :], value_all).astype(low)
        keys = projected_ref[:, lanes_of(1, head)]
        key_all = jnp.concatenate([keys, halo_of(head, tile, key_part)], 0)
        dquery_ref[rows, lanes] = (nn(dscore_s[turn, rows, :], key_all) * scaling).astype(low)
        dkey_t = nn(turned_s[turn, 0, :, rows], dscore_s[turn, rows, rows_local:])
        dvalue_t = nn(turned_s[turn, 1, :, rows], low_s[turn, rows, rows_local:])
        for column, place in enumerate(slots[tile]):
            part = slice(column * TILE, (column + 1) * TILE)
            dkey_s[turn, place] += dkey_t[:, part]
            dvalue_s[turn, place] += dvalue_t[:, part]

    def close_head(head):
        turn = head % 2
        key_rows, value_rows = lanes_of(0, head), lanes_of(1, head)
        dkey = nn(turned_s[turn, 0], dscore_s[turn, :, :rows_local]) * scaling
        dpair_s[key_rows, :rows_local] = dkey.astype(low)
        dpair_s[value_rows, :rows_local] = nn(turned_s[turn, 1], low_s[turn, :, :rows_local]).astype(low)
        for place in range(SLOTS):
            part = slice(rows_local + place * TILE, rows_local + (place + 1) * TILE)
            dpair_s[key_rows, part] = (dkey_s[turn, place] * scaling).astype(low)
            dpair_s[value_rows, part] = dvalue_s[turn, place].astype(low)

    steps = [(head, tile) for head in range(HEADS) for tile in range(tile_count)]
    project(0)
    open_head(0)
    products(*steps[0])
    for place, (head, tile) in enumerate(steps):
        if tile == 2 and head + 1 < HEADS:
            project(head + 1)
        if tile == OPEN_AT and head + 1 < HEADS:
            open_head(head + 1)
        if place + 1 < len(steps):
            products(*steps[place + 1])
        if place > 0:
            finish(*steps[place - 1])
            if tile == 0:
                close_head(head - 1)
        softmax(head, tile)
    finish(*steps[-1])
    close_head(HEADS - 1)
    blocks = width // TILE
    side = place_ref[1]
    for out_ref, half in ((sent_ref, 1 - side), (kept_ref, side)):
        first = pl.multiple_of(half * width, width)
        pairs = nn(dpair_s[pl.ds(first, width), :], normed_s[...])
        store_blocks(out_ref, 0, pairs, blocks)

        @pl.when(half == 0)
        def _():
            store_blocks(out_ref, TILE, nn(normed_t_ref[...], dquery_ref[...]), blocks)

        @pl.when(half != 0)
        def _():
            store_blocks(out_ref, TILE, nn(cotangent_t_ref[...], attended_s[...]), blocks, True)

    for column, back in enumerate(backs):
        first = rows_local + column * CAP * TILE
        part = nn(weight_ref[:, width:], dpair_s[:, first : first + CAP * TILE])
        back[...] = part.astype(jnp.bfloat16).T.reshape(back.shape)
    dpair_ref[...] = dpair_s[:, :rows_local]


def main_scratch(rows_local, width):
    halo_rows = SLOTS * TILE
    all_rows = rows_local + halo_rows
    keys_seen = rows_local + len(OFFSETS) * TILE
    head_width = width // HEADS
    low = jnp.bfloat16
    return [
        pltpu.VMEM((all_rows, width), low),
        pltpu.VMEM((2, halo_rows, 2 * head_width), low),
        pltpu.VMEM((2, rows_local, keys_seen), jnp.float32),
        pltpu.VMEM((2, rows_local, keys_seen), jnp.float32),
        pltpu.VMEM((2, rows_local, keys_seen), low),
        pltpu.VMEM((2, rows_local, keys_seen), low),
        pltpu.VMEM((2, SLOTS, head_width, TILE), jnp.float32),
        pltpu.VMEM((2, SLOTS, head_width, TILE), jnp.float32),
        pltpu.VMEM((2 * width, all_rows), low),
        pltpu.VMEM((rows_local, width), low),
        pltpu.VMEM((2, 2, head_width, rows_local), low),
    ]


def store_blocks(out_ref, first, value, blocks, across=False):
    for row in range(blocks):
        for column in range(blocks):
            block = value[row * TILE : (row + 1) * TILE, column * TILE : (column + 1) * TILE]
            place = column * blocks + row if across else row * blocks + column
            start = place * 2 * TILE + first
            out_ref[start : start + TILE, :] = block.astype(out_ref.dtype)


def output_kernel(flip, place_ref, gathered_ref, *refs):
    qkv_ref, out_ref, pair_s, other_s, sems = refs[-5:]
    width = out_ref.shape[0]
    blocks = width // TILE
    half = place_ref[1] ^ flip
    first = pl.multiple_of((half + 1) * width, width)

    def spot(index):
        return slice(index * TILE, (index + 1) * TILE)

    def strips(row):
        start = pl.multiple_of(first + row * TILE, TILE)
        pair = pltpu.make_async_copy(
            pair_s.at[row], qkv_ref.at[:, pl.ds(start, TILE)], sems.at[row]
        )
        own, sem = other_s.at[row], sems.at[blocks + row]
        left = pltpu.make_async_copy(own, qkv_ref.at[spot(row), :width], sem)
        right = pltpu.make_async_copy(own, out_ref.at[spot(row), :], sem)
        return pair, left, right

    for row in range(blocks):
        pair, left, right = strips(row)
        for column in range(blocks):
            chunk = 2 * (row * blocks + column)
            pair_s[row, spot(column), :] = gathered_ref[spot(chunk), :].astype(jnp.float32)
            other_s[row, :, spot(column)] = gathered_ref[spot(chunk + 1), :].astype(jnp.float32)
        pair.start()
        pl.when(half == 0)(left.start)
        pl.when(half != 0)(right.start)
    for row in range(blocks):
        pair, left, right = strips(row)
        pair.wait()
        pl.when(half == 0)(left.wait)
        pl.when(half != 0)(right.wait)


def input_kernel(
    patches,
    tiles_ref,
    place_ref,
    features_ref,
    cotangent_ref,
    dquery_ref,
    dpair_ref,
    weight_ref,
    back_a,
    back_b,
    back_c,
    back_d,
    out_ref,
    total_s,
):
    position = place_ref[0]
    width = features_ref.shape[1]
    tile_count = features_ref.shape[0] // TILE
    pairs = nn(weight_ref[:, width:], dpair_ref[...])
    total_s[...] = nt(dquery_ref[...], weight_ref[:, :width]) + pairs.T
    for column, (shift_by, back) in enumerate(zip(OFFSETS, (back_a, back_b, back_c, back_d))):
        rows = sent_rows(tiles_ref, position, patches, column, shift_by, tile_count)
        for slot, first in enumerate(rows):
            total_s[pl.ds(first, TILE), :] += back[slot].astype(jnp.float32)
    normed, inverse = normalise(features_ref[...])
    total = total_s[...]
    centred = total - normed * jnp.mean(total * normed, -1, keepdims=True)
    out_ref[...] = (cotangent_ref[...].astype(jnp.float32) + inverse * centred).astype(out_ref.dtype)


def from_behind(value, steps):
    count = lax.axis_size("patch")
    pairs = [(source, (source + steps) % count) for source in range(count)]
    return lax.ppermute(value, "patch", pairs)


def exchange(value, flip, count):
    return lax.ppermute(value, AXES, [(source, source ^ flip) for source in range(count)])


def flips_of(bits):
    return [
        sum(((step >> place) & 1) << bit for place, bit in enumerate(bits))
        for step in range(1 << len(bits))
    ]


def digit_of(index, bits):
    return sum(((index >> bit) & 1) << place for place, bit in enumerate(bits))


def reduce_phase(value, index, bits, count):
    flips = flips_of(bits)
    digit = digit_of(index, bits)
    pieces = value.reshape(len(flips), value.shape[0] // len(flips), value.shape[1])
    received = []
    for step in range(1, len(flips)):
        piece = lax.dynamic_index_in_dim(pieces, digit ^ step, 0, False)
        received.append(exchange(piece, flips[step], count))
    total = lax.dynamic_index_in_dim(pieces, digit, 0, False).astype(jnp.float32)
    for piece in received:
        total = total + piece.astype(jnp.float32)
    return total


def gather_phase(value, index, bits, count):
    flips = flips_of(bits)
    digit = digit_of(index, bits)
    pieces = [value]
    for flip in flips[1:]:
        pieces.append(exchange(value, flip, count))
    stacked = jnp.zeros((len(flips),) + value.shape, value.dtype)
    for step, piece in enumerate(pieces):
        stacked = lax.dynamic_update_index_in_dim(stacked, piece, digit ^ step, 0)
    return stacked.reshape(len(flips) * value.shape[0], value.shape[1])


def first_chunk(index, phases, chunks):
    spread, start = chunks, 0
    for bits in [[0]] + phases:
        spread = spread >> len(bits)
        start = start + digit_of(index, bits) * spread
    return start


def turned(value, first, chunks):
    pairs = value.reshape(-1, 2, TILE, TILE)
    flipped = jnp.swapaxes(pairs, 2, 3)
    chunk = first + jnp.arange(pairs.shape[0], dtype=jnp.int32)
    second = jnp.where((chunk < chunks // 2)[:, None, None], pairs[:, 1], flipped[:, 1])
    return jnp.stack([flipped[:, 0], second], 1).reshape(value.shape)


def on_device(features, cotangent, weight_qkv, weight_out, key_tiles, tile_valid):
    patches = lax.axis_size("patch")
    samples = lax.axis_size("sample")
    count = patches * samples
    position = lax.axis_index("patch").astype(jnp.int32)
    index = position * samples + lax.axis_index("sample").astype(jnp.int32)
    rows_local, width = features.shape[1:]
    rows = features[0]
    grad_rows = cotangent[0]
    low = jnp.bfloat16

    def shape(*dims, kind=low):
        return jax.ShapeDtypeStruct(dims, kind)

    def params(mebibytes):
        return pltpu.CompilerParams(vmem_limit_bytes=mebibytes << 20)

    place = jnp.stack([position, index & 1])
    tiles, valid = key_tiles.T, tile_valid.T
    packed = pl.pallas_call(
        partial(pack_kernel, patches),
        out_shape=[shape(CAP, TILE, width)] * len(OFFSETS),
        in_specs=[SMEM, VMEM],
        out_specs=[VMEM] * len(OFFSETS),
        compiler_params=params(60),
        name="pack",
    )(tiles, rows)
    halos = []
    for piece, shift_by in zip(packed, OFFSETS):
        halos.append(from_behind(piece, -shift_by))
    square = shape(rows_local, width)
    normed_low, normed_t, cotangent_t, projected, grad_attended = pl.pallas_call(
        front_kernel,
        out_shape=[
            square,
            shape(width, rows_local),
            shape(width, rows_local),
            shape(rows_local, 3 * width),
            square,
        ],
        in_specs=[VMEM] * 4,
        out_specs=[VMEM] * 5,
        compiler_params=params(60),
        cost_estimate=pl.CostEstimate(
            flops=8 * rows_local * width * width, bytes_accessed=6 << 20, transcendentals=0
        ),
        name="front",
    )(rows, grad_rows, weight_qkv, weight_out)
    side = index & 1
    block_rows = 4 * width * width // TILE
    outs = pl.pallas_call(
        main_kernel,
        out_shape=[shape(CAP, TILE, width)] * len(OFFSETS)
        + [
            square,
            shape(2 * width, rows_local),
            shape(block_rows // 2, TILE),
            shape(block_rows // 2, TILE),
        ],
        in_specs=[SMEM] * 3 + [VMEM] * 10,
        out_specs=[VMEM] * (len(OFFSETS) + 4),
        scratch_shapes=main_scratch(rows_local, width),
        compiler_params=params(60),
        name="attend",
    )(
        tiles,
        valid,
        place,
        projected,
        grad_attended,
        normed_low,
        normed_t,
        cotangent_t,
        *halos,
        weight_qkv,
    )
    backs, (dquery, dpair, sent, kept) = outs[:4], outs[4:]
    far = [column for column, shift_by in enumerate(OFFSETS) if abs(shift_by) == REACH]
    near = [column for column in range(len(OFFSETS)) if column not in far]
    backs = list(backs)
    returned = {}
    for column in far:
        returned[column] = from_behind(backs[column], OFFSETS[column])
    arrived = exchange(sent, 1, count)
    total = kept.astype(jnp.float32) + arrived.astype(jnp.float32)
    bit_count = count.bit_length() - 1
    phases = [list(range(bit, min(bit + 2, bit_count))) for bit in range(1, bit_count, 2)]
    for turn, bits in enumerate(phases):
        total = reduce_phase(total.astype(low), index, bits, count)
        if turn == 0:
            total, waiting = lax.optimization_barrier((total, [backs[column] for column in near]))
            for column, piece in zip(near, waiting):
                returned[column] = from_behind(piece, OFFSETS[column])
    factor = float(count * rows_local) ** (-0.5)
    total = total * factor
    chunks = block_rows // (2 * TILE)
    whole_chunks = total.shape[0] % (2 * TILE) == 0
    if whole_chunks:
        total = turned(total, first_chunk(index, phases, chunks), chunks)
    gathered = total.astype(low)
    grad_features = None
    for turn, bits in enumerate(phases[::-1]):
        if turn == 1:
            gathered, held = lax.optimization_barrier(
                (gathered, [returned[column] for column in range(len(OFFSETS))])
            )
            grad_features = pl.pallas_call(
                partial(input_kernel, patches),
                out_shape=square,
                in_specs=[SMEM, SMEM] + [VMEM] * 9,
                out_specs=VMEM,
                scratch_shapes=[pltpu.VMEM((rows_local, width), jnp.float32)],
                compiler_params=params(60),
                cost_estimate=pl.CostEstimate(
                    flops=6 * rows_local * width * width, bytes_accessed=6 << 20, transcendentals=0
                ),
                name="inputs",
            )(tiles, place, rows, grad_rows, dquery, dpair, weight_qkv, *held)
        gathered = gather_phase(gathered, index, bits, count)
    other = exchange(gathered, 1, count)
    if not whole_chunks:
        gathered = turned(gathered, side * (chunks // 2), chunks)
        other = turned(other, (1 - side) * (chunks // 2), chunks)

    def outputs(flip, half, *started):
        return pl.pallas_call(
            partial(output_kernel, flip),
            out_shape=[
                shape(width, 3 * width, kind=jnp.float32),
                shape(width, width, kind=jnp.float32),
            ],
            in_specs=[SMEM, VMEM] + [ANY] * len(started),
            out_specs=[ANY] * 2,
            scratch_shapes=[
                pltpu.VMEM((width // TILE, width, TILE), jnp.float32),
                pltpu.VMEM((width // TILE, TILE, width), jnp.float32),
                pltpu.SemaphoreType.DMA((2 * width // TILE,)),
            ],
            input_output_aliases={2: 0, 3: 1} if started else {},
            compiler_params=params(10),
            cost_estimate=pl.CostEstimate(flops=0, bytes_accessed=4 << 20, transcendentals=0),
            name="outputs",
        )(place, half, *started)

    started = outputs(0, gathered)
    grad_qkv, grad_out = outputs(1, other, *started)
    return (grad_features[None], grad_qkv, grad_out)


def solution(mesh):
    placed = (P("sample", "patch", None), P("sample", "patch", None), P(), P(), P(), P())
    return jax.shard_map(
        on_device,
        mesh=mesh,
        in_specs=placed,
        out_specs=(P("sample", "patch", None), P(), P()),
        check_vma=False,
    )
```
